32 devices in a mesh: row: 16 (over z, y, x), col: 2 (over core).
Axes of the slice: x: 2, y: 2, z: 4, core: 2. Of those that a mesh axis runs over, the one named last changes fastest.
Arguments:
- tsdf_prior: float32 [512, 64, 256], P('row', None, 'col'), may hold values from -1 to 1
- prior_weight: float32 [512, 64, 256], P('row', None, 'col'), may hold values from 0.5 to 8
- depth_maps: float32 [16, 131072], P('row'), may hold values from 0 to 64
- confidence: float32 [16, 131072], P('row'), may hold values from 0.2 to 5
- frustum_tiles: int32 [32, 32, 2], P(('row', 'col')), may hold values from -1 to 31, as said below
- pixel_index: int32 [32, 32, 2, 128], P(('row', 'col')), may hold values from 0 to 131071
- conv_weights: bfloat16 [3, 64, 16, 3, 3], replicated, may hold values from -0.5 to 0.5
Outputs:
- refined: float32 [512, 64, 256], P('row', None, 'col')
- new_weight: float32 [512, 64, 256], P('row', None, 'col')
The draws below stay inside these ranges and needn't reach their ends.
Inputs may be any that keep to these rules, and one draw needn't show every extreme that they name: `frustum_tiles`: -1 marks an empty slot; otherwise the entry is one of the owner's 32 tiles, and slot s names a tile from the s-th of 2 equal runs of tile numbers.
All inputs are finite; a program needn't handle non-finite values.
Results may differ from the reference program's by a relative error of at most 0.003.
Values may be sent and summed in bfloat16 or wider, within the bound.
A program may use at most 128 MiB of HBM per device.

```python
import math
import jax
import jax.numpy as jnp
from jax import lax

HB = 64
TC = 128
GR = 32
PIX = 131072
CAP = 2
GROUPS = 4
TRUNC = 4
LAYERS = 3
READERS = 32
OWNERS = 32
MAPS = 16
NGR = 512
NGC = 256
N_ROW = 16
N_COL = 2


def draw_frustum_tiles(key, part):
    first, second, third = jax.random.split(key, 3)
    span = GR // CAP
    layout = (READERS, OWNERS, CAP)
    within = jax.random.randint(first, layout, 0, span)
    chosen = within + span * jnp.arange(CAP, dtype=jnp.int32)
    density = jax.random.randint(second, (READERS, 1, 1), 20, 100)
    rolled = jax.random.randint(third, layout, 0, 100)
    picked = jnp.where(rolled < density, chosen, -1)
    picked = picked.at[0, 0, CAP - 1].set(GR - 1)
    picked = picked.at[0, OWNERS - 1, 0].set(-1)
    return picked.astype(jnp.int32)


def touch_ends(result, own_key, least, largest):
    dims = result.shape
    spot = [jax.random.randint(jax.random.fold_in(own_key, axis), (), 0, dims[axis]) for axis in range(len(dims))]
    result = result.at[tuple(spot)].set(least)
    longest = dims.index(max(dims))
    spot[longest] = (spot[longest] + 1) % dims[longest]
    return result.at[tuple(spot)].set(largest)


def level_of(key, shape, cuts, smallest, largest):
    gain = 1.0
    for axis_at, blocks in cuts:
        draws = jax.random.uniform(jax.random.fold_in(jax.random.fold_in(key, 6), axis_at), (blocks,), jnp.float32, smallest / len(cuts), largest / len(cuts))
        gain = gain * jnp.repeat(jnp.exp(draws), shape[axis_at] // blocks).reshape((-1,) + (1,) * (len(shape) - 1 - axis_at))
    return gain


def normal_values(key, extent, scale, reach, kind=jnp.bfloat16):
    return jnp.clip(scale * jax.random.normal(key, extent, jnp.float32), -reach, reach).astype(kind)


def setup_inputs(seed: int = 0) -> dict:
    key_list = jax.random.split(jax.random.key(seed), 8)
    tsdf_prior = jnp.clip(jax.random.uniform(key_list[0], (NGR, HB, NGC), jnp.float32, -1.0, 1.0) * level_of(key_list[0], (NGR, HB, NGC), ((0, 16), (2, 2)), -0.4, 0.0), -1.0, 1.0)
    prior_weight = jnp.clip(jnp.exp(math.log(8.0) - 2.7725887 * jax.random.uniform(key_list[1], (NGR, HB, NGC), jnp.float32) ** level_of(key_list[1], (NGR, HB, NGC), ((0, 16), (2, 2)), -0.2, 0.2)), 0.5, 8.0)
    depth_maps = jnp.clip(64.0 * jax.random.uniform(key_list[2], (MAPS, PIX), jnp.float32) ** level_of(key_list[2], (MAPS, PIX), ((0, 16),), -0.2, 0.2), 0.0, 64.0)
    confidence = jnp.clip(jnp.exp(math.log(5.0) - 3.218876 * jax.random.uniform(key_list[3], (MAPS, PIX), jnp.float32) ** level_of(key_list[3], (MAPS, PIX), ((0, 16),), -0.2, 0.2)), 0.2, 5.0)
    frustum_tiles = draw_frustum_tiles(jax.random.fold_in(key_list[7], 71), 0)
    pixel_index = touch_ends(jax.random.randint(key_list[5], (READERS, OWNERS, CAP, TC), 0, PIX), jax.random.fold_in(key_list[5], 1), 0, PIX - 1).astype(jnp.int32)
    conv_weights = normal_values(key_list[6], (LAYERS, HB, HB // GROUPS, 3, 3), (9 * HB // GROUPS) ** -0.5, 0.5)
    return {"tsdf_prior": tsdf_prior, "prior_weight": prior_weight, "depth_maps": depth_maps, "confidence": confidence, "frustum_tiles": frustum_tiles, "pixel_index": pixel_index, "conv_weights": conv_weights}


def contributions(blocks, heights, certainty):
    levels = jnp.arange(blocks.shape[-2], dtype=jnp.float32)[:, None]
    scaled = (heights[..., None, :] - levels) / TRUNC
    signed = jnp.clip(scaled, -1.0, 1.0)
    visible = jnp.clip(scaled + 2.0, 0.0, 1.0)
    mismatch = signed - blocks
    observed = certainty[..., None, :] * visible / (1.0 + 4.0 * mismatch * mismatch)
    return observed * signed, observed


def to_tiles(field):
    return field.reshape(N_ROW, GR, HB, N_COL, TC).transpose(0, 3, 1, 2, 4).reshape(N_ROW * N_COL, GR, HB, TC)


def from_tiles(tiled):
    return tiled.reshape(N_ROW, N_COL, GR, HB, TC).transpose(0, 2, 3, 1, 4).reshape(N_ROW * GR, HB, N_COL * TC)


def reference(tsdf_prior, prior_weight, depth_maps, confidence, frustum_tiles, pixel_index, conv_weights):
    tile_view = to_tiles(tsdf_prior)
    owners = jnp.arange(OWNERS, dtype=jnp.int32)[:, None]

    def one_reader(totals, reader):
        wanted = frustum_tiles[reader]
        clamped = jnp.maximum(wanted, 0).astype(jnp.int32)
        blocks = tile_view[owners, clamped]
        map_row = reader // N_COL
        places = pixel_index[reader]
        heights = jnp.take(depth_maps[map_row], places, axis=0)
        certainty = jnp.take(confidence[map_row], places, axis=0)
        weighted, observed = contributions(blocks, heights, certainty)
        present = (wanted >= 0).astype(jnp.float32)[:, :, None, None]
        sum_weighted = totals[0].at[owners, clamped].add(weighted * present)
        sum_observed = totals[1].at[owners, clamped].add(observed * present)
        return (sum_weighted, sum_observed), None

    zeros = jnp.zeros(tile_view.shape, jnp.float32)
    (sum_weighted, sum_observed), _ = lax.scan(one_reader, (zeros, zeros), jnp.arange(READERS, dtype=jnp.int32))
    total_weighted = from_tiles(sum_weighted)
    total_observed = from_tiles(sum_observed)
    joined_field = (prior_weight * tsdf_prior + total_weighted) / (prior_weight + total_observed)
    new_weight = prior_weight + total_observed
    current = joined_field
    for depth_step in range(LAYERS):
        activated = jax.nn.silu(current).astype(jnp.bfloat16)
        activated = lax.optimization_barrier(activated)
        padded = jnp.pad(activated, ((1, 1), (0, 0), (1, 1))).astype(jnp.float32)
        kernel = conv_weights[depth_step].astype(jnp.float32)
        response = lax.conv_general_dilated(padded[None], kernel, (1, 1), "VALID", dimension_numbers=("NHCW", "OIHW", "NHCW"), feature_group_count=GROUPS, precision=lax.Precision.HIGHEST)[0]
        current = current + response
    return current, new_weight
```

```python
import functools

import jax
import jax.numpy as jnp
from jax import lax
from jax.experimental import pallas as pl
from jax.experimental.pallas import tpu as pltpu
from jax.sharding import PartitionSpec as P

GROUPS = 4
TRUNC = 4
LANES = 128
VMEM = pltpu.VMEM
SUB = 8
UNROLL = 256
DEPTH_SCALE = 1023.0
CONF_SCALE = 13000.0


def vmem_specs(count):
    return [pl.BlockSpec(memory_space=VMEM)] * count


def sample_kernel(depth_hbm, conf_hbm, index_hbm, want_hbm, got_ref, ids_ref, small_ref,
                  depth_ref, conf_ref, index_ref, want_ref, table_ref, staged_ref, tiles_ref,
                  in_sems, send_sems, recv_sems, id_send_sems, id_recv_sems):
    owners = got_ref.shape[0]
    cap, own_width = want_hbm.shape
    table_rows = table_ref.shape[0]
    split = lax.axis_size("col")
    my_row, my_col = lax.axis_index("row"), lax.axis_index("col")
    me = my_row * split + my_col
    chips = owners // split
    per_pass = 2 * SUB
    chips_per_pass = per_pass // (split * cap)
    passes = owners * cap // per_pass
    barrier = pltpu.get_barrier_semaphore()

    loads = [pltpu.make_async_copy(src, dst, in_sems.at[i]) for i, (src, dst) in enumerate(
        ((depth_hbm, depth_ref), (conf_hbm, conf_ref), (index_hbm, index_ref), (want_hbm, want_ref)))]
    for load in loads:
        load.start()

    def device(place):
        return (place // split, place % split)

    def peer(k):
        return (me + 1 + k) % owners

    def greet(k, carry):
        pl.semaphore_signal(barrier, inc=1, device_id=device(peer(k)), device_id_type=pl.DeviceIdType.MESH)
        return carry

    lax.fori_loop(0, owners - 1, greet, 0)
    for load in loads:
        load.wait()
    width = tiles_ref.shape[1]
    tiles = want_ref[...]
    if own_width < width:
        tiles = jnp.concatenate([tiles, jnp.full((cap, width - own_width), -1, jnp.int32)], axis=1)
    tiles_ref[...] = tiles

    def pack(i, carry):
        spot = pl.ds(pl.multiple_of(i * 64, 64), 64)
        high = (depth_ref[spot, :] * DEPTH_SCALE + 0.5).astype(jnp.int32) - 32768
        low = (conf_ref[spot, :] * CONF_SCALE + 0.5).astype(jnp.int32)
        table_ref[spot, :] = high * 65536 + low
        return carry

    lax.fori_loop(0, table_rows // 64, pack, 0)
    nothing = jnp.zeros((2, LANES), jnp.int32)
    staged_ref[1, 0:2, :] = nothing
    staged_ref[chips, 6:8, :] = nothing
    pl.semaphore_wait(barrier, owners - 1)

    def id_copy(place, sender):
        return pltpu.make_async_remote_copy(
            src_ref=tiles_ref, dst_ref=ids_ref.at[sender], send_sem=id_send_sems.at[place],
            recv_sem=id_recv_sems.at[sender], device_id=device(place), device_id_type=pl.DeviceIdType.MESH)

    def send_ids(k, carry):
        id_copy(peer(k), me).start()
        return carry

    lax.fori_loop(0, owners - 1, send_ids, 0)
    ids_ref[me] = tiles

    def copy(chip, core, sender):
        return pltpu.make_async_remote_copy(
            src_ref=staged_ref.at[chip + 1], dst_ref=got_ref.at[sender], send_sem=send_sems.at[chip * split + core],
            recv_sem=recv_sems.at[sender], device_id=(chip, core), device_id_type=pl.DeviceIdType.MESH)

    def send(chip):
        @pl.when(chip != my_row)
        def _():
            for core in range(split):
                copy(chip, core, me).start()

        @pl.when(chip == my_row)
        def _():
            copy(chip, 1 - my_col, me).start()
            got_ref[me] = staged_ref[chip + 1]

    my_pass = my_row // chips_per_pass

    def one_pass(k, carry):
        p = (my_pass + 1 + k) % passes
        lanes, rows = [], []
        for half in range(2):
            index = index_ref[pl.ds(pl.multiple_of(p * per_pass + half * SUB, SUB), SUB), :]
            lanes.append(jnp.bitwise_and(index, LANES - 1))
            rows.append(jnp.right_shift(index, 7))

        def block(b, found):
            found = list(found)
            base = b * UNROLL
            left = [row - base for row in rows]
            for u in range(UNROLL):
                line = jnp.broadcast_to(table_ref[pl.ds(base + u, 1), :], (SUB, LANES))
                for half in range(2):
                    here = jnp.take_along_axis(line, lanes[half], axis=1)
                    found[half] = jnp.where(left[half] == u, here, found[half])
            return tuple(found)

        start = (jnp.zeros((SUB, LANES), jnp.int32),) * 2
        found = lax.fori_loop(0, table_rows // UNROLL, block, start)
        first = p * chips_per_pass
        for i in range(chips_per_pass):
            own = found[i // 2][4 * (i % 2) : 4 * (i % 2) + 4]
            chip = first + i
            staged_ref[chip + 1, 2:6, :] = own
            staged_ref[chip + 2, 0:1, :] = own[1:2]
            staged_ref[chip + 2, 1:2, :] = own[3:4]
            staged_ref[chip, 6:7, :] = own[0:1]
            staged_ref[chip, 7:8, :] = own[2:3]
        final = k == passes - 1

        @pl.when((k >= 1) & (p >= 1))
        def _():
            send(first - 1)
            send(first)

        @pl.when(p == 0)
        def _():
            send(0)

        for i in range(1, chips_per_pass - 1):
            send(first + i)

        @pl.when(p == passes - 1)
        def _():
            send(chips - 1)

        @pl.when((k == passes - 1) & (p < passes - 1))
        def _():
            send(first + chips_per_pass - 1)
            send(first + chips_per_pass)

        return carry

    lax.fori_loop(0, passes, one_pass, 0)

    def drain_ids(k, carry):
        place = peer(k)
        id_copy(place, me).wait_send()
        id_copy(place, place).wait_recv()
        return carry

    lax.fori_loop(0, owners - 1, drain_ids, 0)
    lane = lax.broadcasted_iota(jnp.int32, (SUB, LANES), 1)
    other = my_row * split + 1 - my_col
    spots = (me, other, me - split, other - split, me + split, other + split)
    spot = jnp.zeros((SUB, LANES), jnp.int32)
    for j, place in enumerate(spots):
        spot = jnp.where(lane == j, jnp.minimum(jnp.maximum(place, 0), owners - 1), spot)
    flat = []
    for q in range(0, owners, SUB // cap):
        part = jnp.concatenate([ids_ref[q + i] for i in range(SUB // cap)], axis=0)
        flat.append(jnp.take_along_axis(part, spot, axis=1))
    wanted = jnp.concatenate(flat, axis=0).astype(jnp.float32)
    for at in range(0, owners * cap, LANES):
        piece = wanted[at : at + LANES]
        if piece.shape[0] < LANES:
            piece = jnp.concatenate([piece, jnp.zeros((LANES - piece.shape[0], LANES), jnp.float32)], axis=0)
        small_ref[:, at : at + LANES] = piece.T[0:SUB].astype(jnp.int32)

    def drain(k, carry):
        place = peer(k)
        copy(place // split, place % split, me).wait_send()
        copy(place // split, place % split, place).wait_recv()
        return carry

    lax.fori_loop(0, owners - 1, drain, 0)


def join_kernel(halo, ids_ref, side_ref, got_ref, prior_ref, weight_ref, joined_ref, total_ref, packed_ref):
    tiles, bins, cols = prior_ref.shape
    readers = got_ref.shape[0]
    cap = 2
    side = side_ref[0]

    def begin(t, carry):
        weight = weight_ref[t]
        total_ref[t] = weight
        joined_ref[t] = weight * prior_ref[t]
        return carry

    lax.fori_loop(0, tiles, begin, 0, unroll=4)
    levels = lax.broadcasted_iota(jnp.int32, (bins, cols), 0).astype(jnp.float32)

    batch = 2

    def add(step, carry):
        terms = []
        for one in range(batch):
            reader = step * batch + one
            for s in range(cap):
                listed = ids_ref[0, reader * cap + s]
                tile = jnp.maximum(listed, 0)
                word = got_ref[reader, pl.ds(2 + 2 * side + s, 1), :]
                height = (jnp.right_shift(word, 16) + 32768).astype(jnp.float32) * (1.0 / DEPTH_SCALE)
                sure = jnp.bitwise_and(word, 65535).astype(jnp.float32) * (1.0 / CONF_SCALE)
                sure = jnp.where(listed >= 0, sure, 0.0)
                scaled = (height - levels) * (1.0 / TRUNC)
                signed = jnp.clip(scaled, -1.0, 1.0)
                visible = jnp.clip(scaled + 2.0, 0.0, 1.0)
                miss = signed - prior_ref[tile]
                observed = sure * visible / (1.0 + 4.0 * miss * miss)
                terms.append((tile, observed, observed * signed))
        for tile, observed, weighted in terms:
            total_ref[tile] += observed
            joined_ref[tile] += weighted
        return carry

    lax.fori_loop(0, readers // batch, add, 0)
    place = lax.broadcasted_iota(jnp.int32, (bins, cols), 1)
    first = side_ref[0] == 0

    def finish(t, packed):
        value = joined_ref[t] / total_ref[t]
        joined_ref[t] = value
        shift = halo * t + jnp.where(first, halo, 0)
        shift = jnp.where(shift >= cols, shift - cols, shift)
        moved = pltpu.roll(value, shift, 1)
        here = (place >= halo * t) & (place < halo * t + halo)
        return jnp.where(here, moved, packed)

    packed_ref[...] = lax.fori_loop(0, tiles, finish, jnp.zeros((bins, cols), jnp.float32), unroll=4)


def refine_kernel(layers, joined_ref, packed_ref, kernel_ref, out_ref,
                  edge_rows, edge_cols, cur_ref, even_ref, odd_ref, weights_ref, send_sems, recv_sems):
    tiles, bins, cols = joined_ref.shape
    halo = layers
    row, col = lax.axis_index("row"), lax.axis_index("col")
    has_up = row > 0
    has_down = row < lax.axis_size("row") - 1
    other = 1 - col
    barrier = pltpu.get_barrier_semaphore()

    def greet(device):
        pl.semaphore_signal(barrier, inc=1, device_id=device, device_id_type=pl.DeviceIdType.MESH)

    greet((row, other))

    @pl.when(has_up)
    def _():
        greet((row - 1, col))
        greet((row - 1, other))

    @pl.when(has_down)
    def _():
        greet((row + 1, col))
        greet((row + 1, other))

    pl.semaphore_wait(barrier, 1 + 2 * has_up.astype(jnp.int32) + 2 * has_down.astype(jnp.int32))

    def copy(source, target, slot, device):
        return pltpu.make_async_remote_copy(
            src_ref=source, dst_ref=target, send_sem=send_sems.at[slot], recv_sem=recv_sems.at[slot],
            device_id=device, device_id_type=pl.DeviceIdType.MESH)

    leading = joined_ref.at[0:halo]
    trailing = joined_ref.at[tiles - halo : tiles]
    to_side = copy(packed_ref, edge_cols.at[0], 2, (row, other))
    to_down = copy(trailing, edge_rows.at[0], 0, (row + 1, col))
    to_down_side = copy(packed_ref, edge_cols.at[1], 3, (row + 1, other))
    to_up = copy(leading, edge_rows.at[1], 1, (row - 1, col))
    to_up_side = copy(packed_ref, edge_cols.at[2], 4, (row - 1, other))
    to_side.start()

    @pl.when(has_up)
    def _():
        to_up.start()
        to_up_side.start()

    @pl.when(has_down)
    def _():
        to_down.start()
        to_down_side.start()

    lane = lax.broadcasted_iota(jnp.int32, (bins, cols), 1)
    first = col == 0
    low = jnp.where(first, 0, cols - halo)
    in_edge = (lane >= low) & (lane < low + halo)

    def silu(v):
        half = 0.5 * v
        return (half + half * jnp.tanh(half)).astype(jnp.bfloat16)

    def unpack(tile, at):
        shift = jnp.where(first, 0, cols - halo) - halo * at
        shift = jnp.where(shift < 0, shift + cols, shift)
        return jnp.where(in_edge, pltpu.roll(tile, shift, 1), 0.0)

    def put_main(r, main):
        at = pl.multiple_of(r * bins, bins)
        cur_ref[pl.ds(at, bins), 0:cols] = main
        even_ref[pl.ds(at, bins), 0:cols] = silu(main)

    def put_side(r, side):
        at = pl.multiple_of(r * bins, bins)
        cur_ref[pl.ds(at, bins), cols : 2 * cols] = side
        even_ref[pl.ds(at, bins), cols : 2 * cols] = silu(side)

    def put(r, main, side):
        put_main(r, main)
        put_side(r, side)

    def fill_main(t, carry):
        put_main(t + halo, joined_ref[t])
        return carry

    def fill_side(t, carry):
        put_side(t + halo, unpack(edge_cols[0], t))
        return carry

    lax.fori_loop(0, tiles, fill_main, 0, unroll=4)
    group_in = lax.broadcasted_iota(jnp.int32, (bins, bins), 0) // (bins // GROUPS)
    group_out = lax.broadcasted_iota(jnp.int32, (bins, bins), 1) // (bins // GROUPS)
    empty = jnp.zeros((bins, bins), jnp.bfloat16)

    def widen(layer, carry):
        for dc in range(3):
            blocks = []
            for dr in range(3):
                own = kernel_ref[layer, dr, dc].astype(jnp.float32)
                full = jnp.where(group_in == group_out, jnp.concatenate([own] * GROUPS, axis=0), 0.0)
                blocks.append(full.T.astype(jnp.bfloat16))
            weights_ref[layer, dc * bins : (dc + 1) * bins, :] = jnp.concatenate(blocks + [empty], axis=1)
            weights_ref[layer, (3 + dc) * bins : (4 + dc) * bins, :] = jnp.concatenate([empty] + blocks, axis=1)
        return carry

    lax.fori_loop(0, layers, widen, 0)
    to_side.wait_recv()
    lax.fori_loop(0, tiles, fill_side, 0, unroll=4)
    nothing = jnp.zeros((bins, cols), jnp.float32)
    outer = jnp.zeros((bins, 2 * cols), jnp.bfloat16)
    odd_ref[0:bins, :] = outer
    odd_ref[(tiles + 2 * halo - 1) * bins : (tiles + 2 * halo) * bins, :] = outer

    @pl.when(has_up)
    def _():
        to_down.wait_recv()
        to_down_side.wait_recv()
        for i in range(halo):
            put(i, edge_rows[0, i], unpack(edge_cols[1], tiles - halo + i))

    @pl.when(jnp.logical_not(has_up))
    def _():
        for i in range(halo):
            put(i, nothing, nothing)

    @pl.when(has_down)
    def _():
        to_up.wait_recv()
        to_up_side.wait_recv()
        for i in range(halo):
            put(tiles + halo + i, edge_rows[1, i], unpack(edge_cols[2], i))

    @pl.when(jnp.logical_not(has_down))
    def _():
        for i in range(halo):
            put(tiles + halo + i, nothing, nothing)

    wide_lane = lax.broadcasted_iota(jnp.int32, (bins, 2 * cols), 1)
    wide_low = jnp.where(first, 0, 2 * cols - halo)
    col_inside = (wide_lane < cols) | ((wide_lane >= jnp.where(first, cols, 2 * cols - halo))
                                       & (wide_lane < jnp.where(first, cols + halo, 2 * cols)))
    top = jnp.where(has_up, 0, halo)
    bottom = jnp.where(has_down, tiles + 2 * halo, tiles + halo)
    pair = 2
    batch = 2
    stride = pair * batch
    for layer in range(layers):
        now_ref, later_ref = (even_ref, odd_ref) if layer % 2 == 0 else (odd_ref, even_ref)
        last = layer == layers - 1
        begin = halo if last else 1
        end = tiles + halo if last else tiles + 2 * halo - 1

        def rows(step, carry):
            base = begin + step * stride
            values = []
            for one in range(batch):
                at = (base + one * pair) * bins
                window = now_ref[pl.ds(pl.multiple_of(at - bins, bins), (pair + 2) * bins), :]
                parts = jnp.dot(weights_ref[layer], window, preferred_element_type=jnp.float32)
                for j in range(pair):
                    part = parts[3 * bins * j : 3 * bins * (j + 1)]
                    response = (pltpu.roll(part[0:bins], 1, 1) + part[bins : 2 * bins]
                                + pltpu.roll(part[2 * bins : 3 * bins], 2 * cols - 1, 1))
                    spot = pl.ds(pl.multiple_of(at + j * bins, bins), bins)
                    r = base + one * pair + j
                    if last:
                        values.append((r, spot, cur_ref[spot, 0:cols] + response[:, 0:cols]))
                    else:
                        values.append((r, spot, cur_ref[spot, :] + response))
            for r, spot, value in values:
                if last:
                    out_ref[r - halo] = value
                else:
                    cur_ref[spot, :] = value
                    keep = col_inside & (r >= top) & (r < bottom)
                    later_ref[spot, :] = silu(jnp.where(keep, value, 0.0))
            return carry

        lax.fori_loop(0, (end - begin) // stride, rows, 0)

    to_side.wait_send()

    @pl.when(has_up)
    def _():
        to_up.wait_send()
        to_up_side.wait_send()

    @pl.when(has_down)
    def _():
        to_down.wait_send()
        to_down_side.wait_send()


def on_device(
    tsdf_prior, prior_weight, depth_maps, confidence, frustum_tiles, pixel_index, conv_weights
):
    tiles, bins, cols = tsdf_prior.shape
    owners, cap = frustum_tiles.shape[1:]
    layers = conv_weights.shape[0]
    pixels = depth_maps.shape[1]
    f32 = jnp.float32
    width = -(-owners // LANES) * LANES
    small = -(-owners * cap // LANES) * LANES
    i32 = jnp.int32
    hbm = pl.BlockSpec(memory_space=pltpu.HBM)
    got, _, ids = pl.pallas_call(
        sample_kernel,
        out_shape=(jax.ShapeDtypeStruct((owners, SUB, LANES), i32),
                   jax.ShapeDtypeStruct((owners, cap, width), i32),
                   jax.ShapeDtypeStruct((SUB, small), i32)),
        in_specs=[hbm] * 4,
        out_specs=tuple(vmem_specs(3)),
        scratch_shapes=[
            VMEM((pixels // LANES, LANES), f32),
            VMEM((pixels // LANES, LANES), f32),
            VMEM((owners * cap, LANES), i32),
            VMEM((cap, owners), i32),
            VMEM((pixels // LANES, LANES), i32),
            VMEM((owners // 2 + 2, SUB, LANES), i32),
            VMEM((cap, width), i32),
            pltpu.SemaphoreType.DMA((4,)),
            pltpu.SemaphoreType.DMA((owners,)),
            pltpu.SemaphoreType.DMA((owners,)),
            pltpu.SemaphoreType.DMA((owners,)),
            pltpu.SemaphoreType.DMA((owners,)),
        ],
        compiler_params=pltpu.CompilerParams(collective_id=1, has_side_effects=True, vmem_limit_bytes=20 << 20),
        name="sample",
    )(depth_maps.reshape(-1, LANES), confidence.reshape(-1, LANES), pixel_index.reshape(-1, LANES), frustum_tiles[0].T)
    side = lax.axis_index("col").astype(jnp.int32).reshape(1)
    field = jax.ShapeDtypeStruct((tiles, bins, cols), f32)
    joined, new_weight, packed = pl.pallas_call(
        functools.partial(join_kernel, layers),
        out_shape=(field, field, jax.ShapeDtypeStruct((bins, cols), f32)),
        in_specs=[pl.BlockSpec(memory_space=pltpu.SMEM)] * 2 + vmem_specs(3),
        out_specs=tuple(vmem_specs(3)),
        compiler_params=pltpu.CompilerParams(vmem_limit_bytes=20 << 20),
        name="join",
    )(ids, side, got, tsdf_prior, prior_weight)
    total_rows = tiles + 2 * layers
    refined = pl.pallas_call(
        functools.partial(refine_kernel, layers),
        out_shape=field,
        in_specs=vmem_specs(3),
        out_specs=pl.BlockSpec(memory_space=VMEM),
        scratch_shapes=[
            VMEM((2, layers, bins, cols), f32),
            VMEM((3, bins, cols), f32),
            VMEM((total_rows * bins, 2 * cols), f32),
            VMEM((total_rows * bins, 2 * cols), jnp.bfloat16),
            VMEM((total_rows * bins, 2 * cols), jnp.bfloat16),
            VMEM((layers, 6 * bins, 4 * bins), jnp.bfloat16),
            pltpu.SemaphoreType.DMA((5,)),
            pltpu.SemaphoreType.DMA((5,)),
        ],
        compiler_params=pltpu.CompilerParams(collective_id=0, has_side_effects=True, vmem_limit_bytes=20 << 20),
        name="refine",
    )(joined, packed, conv_weights.transpose(0, 3, 4, 2, 1))
    return (refined, new_weight)


def solution(mesh):
    placed = (
        P("row", None, "col"),
        P("row", None, "col"),
        P("row", None),
        P("row", None),
        P(("row", "col"), None, None),
        P(("row", "col"), None, None, None),
        P(),
    )
    return jax.shard_map(
        on_device,
        mesh=mesh,
        in_specs=placed,
        out_specs=(P("row", None, "col"), P("row", None, "col")),
        check_vma=False,
    )
```

```python
import functools

import jax
import jax.numpy as jnp
from jax import lax
from jax.experimental import pallas as pl
from jax.experimental.pallas import tpu as pltpu
from jax.sharding import PartitionSpec as P

GROUPS = 4
TRUNC = 4
LANES = 128
VMEM = pltpu.VMEM
UNROLL_ROWS = 4


def vmem_specs(count):
    return [pl.BlockSpec(memory_space=VMEM)] * count


def sample_kernel(places_hbm, depth_hbm, conf_hbm, want_hbm, got_ref, ids_ref,
                  places_ref, depth_ref, conf_ref, want_ref, table_ref, staged_ref,
                  in_sems, send_sems, recv_sems):
    loads = [pltpu.make_async_copy(src, dst, in_sems.at[i]) for i, (src, dst) in enumerate(
        ((depth_hbm, depth_ref), (conf_hbm, conf_ref), (places_hbm, places_ref), (want_hbm, want_ref)))]
    for load in loads:
        load.start()
    owners, cap, _ = places_ref.shape
    depth_rows = depth_ref.shape[0]
    split = lax.axis_size("col")
    me = lax.axis_index("row") * split + lax.axis_index("col")
    barrier = pltpu.get_barrier_semaphore()

    def wrapped(place):
        return jnp.where(place >= owners, place - owners, place)

    def coordinates(place):
        return (place // split, place % split)

    def greet(k, carry):
        pl.semaphore_signal(barrier, inc=1, device_id=coordinates(wrapped(me + 1 + k)),
                            device_id_type=pl.DeviceIdType.MESH)
        return carry

    lax.fori_loop(0, owners - 1, greet, 0)
    for load in loads:
        load.wait()
    for at in range(0, depth_rows, LANES):
        block = depth_ref[at : at + LANES, :].T
        high = block.astype(jnp.bfloat16)
        table_ref[0:LANES, at : at + LANES] = high
        table_ref[LANES : 2 * LANES, at : at + LANES] = (block - high.astype(jnp.float32)).astype(jnp.bfloat16)
        table_ref[2 * LANES : 3 * LANES, at : at + LANES] = conf_ref[at : at + LANES, :].T.astype(jnp.bfloat16)
    want = want_ref[...].astype(jnp.float32)
    listed_by = lax.broadcasted_iota(jnp.int32, want.shape, 1)
    wide = cap * LANES

    def compute(k):
        owner = wrapped(me + 1 + k)
        listed = places_ref[owner]
        index = jnp.concatenate([listed[s : s + 1, :] for s in range(cap)], axis=1)
        row = index // LANES
        lane = index % LANES
        hot = (lax.broadcasted_iota(jnp.int32, (depth_rows, wide), 0) == row)
        hot = hot.astype(jnp.float32).astype(jnp.bfloat16)
        found = jnp.dot(table_ref[...], hot, preferred_element_type=jnp.float32)
        chosen = lax.broadcasted_iota(jnp.int32, (LANES, wide), 0) == lane
        results = []
        for value in (found[0:LANES] + found[LANES : 2 * LANES], found[2 * LANES : 3 * LANES]):
            value = jnp.sum(jnp.where(chosen, value, 0.0), axis=0, keepdims=True)
            results += [value[:, s * LANES : (s + 1) * LANES] for s in range(cap)]
        tile = jnp.sum(jnp.where(listed_by == owner, want, 0.0), axis=1, keepdims=True)
        results.append(jnp.broadcast_to(tile, (cap, LANES)))
        return owner, jnp.concatenate(results, axis=0)

    def copy(k):
        owner = wrapped(me + 1 + k)
        return pltpu.make_async_remote_copy(
            src_ref=staged_ref.at[owner], dst_ref=got_ref.at[me],
            send_sem=send_sems.at[k], recv_sem=recv_sems.at[k],
            device_id=coordinates(owner), device_id_type=pl.DeviceIdType.MESH)

    def arrival(k):
        sender = wrapped(me + owners - 1 - k)
        return pltpu.make_async_remote_copy(
            src_ref=staged_ref.at[sender], dst_ref=got_ref.at[sender],
            send_sem=send_sems.at[k], recv_sem=recv_sems.at[k],
            device_id=coordinates(sender), device_id_type=pl.DeviceIdType.MESH)

    def stage(k):
        pairs = [compute(k), compute(k + 1)]
        for owner, value in pairs:
            staged_ref[owner] = value

    stage(0)
    pl.semaphore_wait(barrier, owners - 1)

    def step(p, carry):
        copy(2 * p - 2).start()
        copy(2 * p - 1).start()
        stage(2 * p)
        return carry

    lax.fori_loop(1, owners // 2, step, 0)
    copy(owners - 2).start()
    got_ref[me] = staged_ref[me]

    def drain(k, carry):
        copy(k).wait_send()
        arrival(k).wait_recv()
        return carry

    lax.fori_loop(0, owners - 1, drain, 0)
    ids_ref[...] = got_ref[:, 2 * cap : 3 * cap, :].astype(jnp.int32)


def join_kernel(halo, ids_ref, side_ref, got_ref, prior_ref, weight_ref, joined_ref, total_ref, packed_ref):
    tiles, bins, cols = prior_ref.shape
    readers, rows, _ = got_ref.shape
    cap = rows // 3

    def begin(t, carry):
        weight = weight_ref[t]
        total_ref[t] = weight
        joined_ref[t] = weight * prior_ref[t]
        return carry

    lax.fori_loop(0, tiles, begin, 0, unroll=4)
    levels = lax.broadcasted_iota(jnp.int32, (bins, cols), 0).astype(jnp.float32)

    batch = 2

    def add(step, carry):
        terms = []
        for one in range(batch):
            reader = step * batch + one
            for s in range(cap):
                listed = ids_ref[reader, s, 0]
                tile = jnp.maximum(listed, 0)
                height = got_ref[reader, s : s + 1, :]
                sure = got_ref[reader, cap + s : cap + s + 1, :]
                sure = jnp.where(listed >= 0, sure, 0.0)
                scaled = (height - levels) * (1.0 / TRUNC)
                signed = jnp.clip(scaled, -1.0, 1.0)
                visible = jnp.clip(scaled + 2.0, 0.0, 1.0)
                miss = signed - prior_ref[tile]
                observed = sure * visible / (1.0 + 4.0 * miss * miss)
                terms.append((tile, observed, observed * signed))
        for tile, observed, weighted in terms:
            total_ref[tile] += observed
            joined_ref[tile] += weighted
        return carry

    lax.fori_loop(0, readers // batch, add, 0)
    place = lax.broadcasted_iota(jnp.int32, (bins, cols), 1)
    first = side_ref[0] == 0

    def finish(t, packed):
        value = joined_ref[t] / total_ref[t]
        joined_ref[t] = value
        shift = halo * t + jnp.where(first, halo, 0)
        shift = jnp.where(shift >= cols, shift - cols, shift)
        moved = pltpu.roll(value, shift, 1)
        here = (place >= halo * t) & (place < halo * t + halo)
        return jnp.where(here, moved, packed)

    packed_ref[...] = lax.fori_loop(0, tiles, finish, jnp.zeros((bins, cols), jnp.float32), unroll=4)


def refine_kernel(layers, joined_ref, packed_ref, kernel_ref, out_ref,
                  edge_rows, edge_cols, cur_ref, even_ref, odd_ref, weights_ref, side_weights_ref,
                  side_ref, gap_ref, send_sems, recv_sems):
    tiles, bins, cols = joined_ref.shape
    halo = layers
    total = tiles + 2 * halo
    row, col = lax.axis_index("row"), lax.axis_index("col")
    has_up = row > 0
    has_down = row < lax.axis_size("row") - 1
    other = 1 - col
    barrier = pltpu.get_barrier_semaphore()

    def greet(device):
        pl.semaphore_signal(barrier, inc=1, device_id=device, device_id_type=pl.DeviceIdType.MESH)

    greet((row, other))

    @pl.when(has_up)
    def _():
        greet((row - 1, col))
        greet((row - 1, other))

    @pl.when(has_down)
    def _():
        greet((row + 1, col))
        greet((row + 1, other))

    pl.semaphore_wait(barrier, 1 + 2 * has_up.astype(jnp.int32) + 2 * has_down.astype(jnp.int32))

    def copy(source, target, slot, device):
        return pltpu.make_async_remote_copy(
            src_ref=source, dst_ref=target, send_sem=send_sems.at[slot], recv_sem=recv_sems.at[slot],
            device_id=device, device_id_type=pl.DeviceIdType.MESH)

    leading = joined_ref.at[0:halo]
    trailing = joined_ref.at[tiles - halo : tiles]
    to_side = copy(packed_ref, edge_cols.at[0], 2, (row, other))
    to_down = [copy(packed_ref, edge_cols.at[1], 3, (row + 1, other)),
               copy(packed_ref, edge_cols.at[3], 5, (row + 1, col)),
               copy(trailing, edge_rows.at[0], 0, (row + 1, col))]
    to_up = [copy(packed_ref, edge_cols.at[2], 4, (row - 1, other)),
             copy(packed_ref, edge_cols.at[4], 6, (row - 1, col)),
             copy(leading, edge_rows.at[1], 1, (row - 1, col))]
    to_side.start()

    @pl.when(has_up)
    def _():
        for one in to_up:
            one.start()

    @pl.when(has_down)
    def _():
        for one in to_down:
            one.start()

    first = col == 0
    near, far = jnp.where(first, cols - 1, 0), jnp.where(first, 0, cols - 1)
    inward = jnp.where(first, 2, 0)
    lane = lax.broadcasted_iota(jnp.int32, (bins, cols), 1)
    is_near, is_far = lane == near, lane == far

    def silu(v):
        half = 0.5 * v
        return half + half * jnp.tanh(half)

    def put(r, value):
        spot = pl.ds(pl.multiple_of(r * bins, bins), bins)
        cur_ref[spot, :] = value
        even_ref[spot, :] = silu(value).astype(jnp.bfloat16)

    group_in = lax.broadcasted_iota(jnp.int32, (bins, bins), 0) // (bins // GROUPS)
    group_out = lax.broadcasted_iota(jnp.int32, (bins, bins), 1) // (bins // GROUPS)
    empty = jnp.zeros((bins, bins), jnp.bfloat16)

    def widen(layer, carry):
        def dense(dr, dc):
            own = kernel_ref[layer, dr, dc].astype(jnp.float32)
            full = jnp.where(group_in == group_out, jnp.concatenate([own] * GROUPS, axis=0), 0.0)
            return full.T.astype(jnp.bfloat16)

        for at, dc in ((0, 2 - inward), (1, 1), (2, inward)):
            blocks = [dense(dr, dc) for dr in range(3)]
            weights_ref[layer, at * bins : (at + 1) * bins, :] = jnp.concatenate(blocks + [empty], axis=1)
            weights_ref[layer, (3 + at) * bins : (4 + at) * bins, :] = jnp.concatenate([empty] + blocks, axis=1)
        below = [dense(dr, inward) if dc == 1 else empty for dr in range(3) for dc in range(3)]
        side_weights_ref[layer, 0:bins, :] = jnp.concatenate(
            [dense(dr, dc) for dr in range(3) for dc in range(3)], axis=1)
        side_weights_ref[layer, bins : 2 * bins, :] = jnp.concatenate(below, axis=1)
        return carry

    def fill(t, carry):
        put(t + halo, joined_ref[t])
        return carry

    lax.fori_loop(0, layers, widen, 0)
    lax.fori_loop(0, tiles, fill, 0, unroll=4)

    wide = side_ref.shape[1]
    span = 2 * halo - 1
    half_lane = [lane + at for at in range(0, wide, cols)]
    place = [one // span for one in half_lane]
    spot_in = [one % span for one in half_lane]
    mine_low, mine_high = jnp.where(first, 0, halo), jnp.where(first, halo - 1, span)
    mine = [(one >= mine_low) & (one < mine_high) for one in spot_in]
    mine_col = jnp.where(first, 1, -halo)
    side_col = jnp.where(first, 1 - halo, 0)
    shift_in = [one + jnp.where(m, mine_col, side_col) for one, m in zip(spot_in, mine)]

    def collect(own, neighbour, h, offset, low, high):
        source = (place[h] - offset) * halo + shift_in[h]
        source = jnp.minimum(jnp.maximum(source, 0), cols - 1)
        value = jnp.where(mine[h], jnp.take_along_axis(own, source, axis=1),
                          jnp.take_along_axis(neighbour, source, axis=1))
        return value, (place[h] >= low) & (place[h] < high)

    to_side.wait_recv()
    for h in range(len(place)):
        value, here = collect(packed_ref[...], edge_cols[0], h, halo, halo, halo + tiles)
        side_ref[:, h * cols : (h + 1) * cols] = jnp.where(here, value, 0.0)
    outer = jnp.zeros((bins, cols), jnp.bfloat16)
    odd_ref[0:bins, :] = outer
    odd_ref[(total - 1) * bins : total * bins, :] = outer
    nothing = jnp.zeros((bins, cols), jnp.float32)

    def join_side(own, neighbour, offset, low, high):
        for h in range(len(place)):
            if low < (h + 1) * cols // span + 1 and high > h * cols // span:
                value, here = collect(own, neighbour, h, offset, low, high)
                part = side_ref[:, h * cols : (h + 1) * cols]
                side_ref[:, h * cols : (h + 1) * cols] = jnp.where(here, value, part)

    @pl.when(has_up)
    def _():
        for one in to_down:
            one.wait_recv()
        join_side(edge_cols[3], edge_cols[1], halo - tiles, 0, halo)
        for i in range(halo):
            put(i, edge_rows[0, i])

    @pl.when(jnp.logical_not(has_up))
    def _():
        for i in range(halo):
            put(i, nothing)

    @pl.when(has_down)
    def _():
        for one in to_up:
            one.wait_recv()
        join_side(edge_cols[4], edge_cols[2], halo + tiles, halo + tiles, total)
        for i in range(halo):
            put(tiles + halo + i, edge_rows[1, i])

    @pl.when(jnp.logical_not(has_down))
    def _():
        for i in range(halo):
            put(tiles + halo + i, nothing)

    wide_place = lax.broadcasted_iota(jnp.int32, (bins, wide), 1) // span
    inside = ((wide_place >= jnp.where(has_up, 0, halo))
              & (wide_place < jnp.where(has_down, total, tiles + halo)))
    middle = span // 2

    def side_step(layer, carry):
        now = side_ref[...]
        active = silu(now)
        shifted = []
        for dr in range(-1, 2):
            for dc in range(-1, 2):
                offset = (-(span * dr + dc)) % wide
                moved = active if offset == 0 else pltpu.roll(active, offset, 1)
                shifted.append(moved.astype(jnp.bfloat16))
        result = jnp.dot(side_weights_ref[layer], jnp.concatenate(shifted, axis=0),
                         preferred_element_type=jnp.float32)
        side_ref[...] = jnp.where(inside, now + result[0:bins], 0.0)
        gap = nothing
        for h in range(len(place)):
            source = lane * span + middle - h * cols
            ok = (source >= 0) & (source < cols)
            moved = jnp.take_along_axis(result[bins : 2 * bins, h * cols : (h + 1) * cols],
                                        jnp.minimum(jnp.maximum(source, 0), cols - 1), axis=1)
            gap = jnp.where(ok, moved, gap)
        gap_ref[layer] = gap
        return carry

    lax.fori_loop(0, layers, side_step, 0)
    inner_shift, outer_shift = jnp.where(first, cols - 1, 1), jnp.where(first, 1, cols - 1)
    pair = 2
    stride = 2 * pair
    for layer in range(layers):
        now_ref, later_ref = (even_ref, odd_ref) if layer % 2 == 0 else (odd_ref, even_ref)
        last = layer == layers - 1
        begin = halo if last else 1
        end = tiles + halo if last else total - 1

        steps = (end - begin) // stride
        unroll = max(u for u in range(1, UNROLL_ROWS + 1) if steps % u == 0)

        def store(r, spot, value):
            if last:
                out_ref[r - halo] = value
            else:
                cur_ref[spot, :] = value
                later_ref[spot, :] = silu(value).astype(jnp.bfloat16)

        def rows(step, carry):
            for one in range(unroll):
                base = begin + step * (stride * unroll) + one * stride
                at = base * bins
                span_rows = (pair + 2) * bins
                window = jnp.concatenate(
                    [now_ref[pl.ds(pl.multiple_of(at - bins + h * pair * bins, bins), span_rows), :]
                     for h in range(2)], axis=1)
                parts = jnp.dot(weights_ref[layer], window, preferred_element_type=jnp.float32)
                for h in range(2):
                    for j in range(pair):
                        part = parts[3 * bins * j : 3 * bins * (j + 1), h * cols : (h + 1) * cols]
                        r = base + h * pair + j
                        shift = near - r
                        gap = pltpu.roll(gap_ref[layer], jnp.where(shift < 0, shift + cols, shift), 1)
                        response = (jnp.where(is_far, 0.0, pltpu.roll(part[0:bins], outer_shift, 1))
                                    + part[bins : 2 * bins]
                                    + jnp.where(is_near, gap, pltpu.roll(part[2 * bins : 3 * bins], inner_shift, 1)))
                        spot = pl.ds(pl.multiple_of(r * bins, bins), bins)
                        value = cur_ref[spot, :] + response
                        store(r, spot, value)
            return carry

        lax.fori_loop(0, steps // unroll, rows, 0)
        if not last:
            blank = jnp.zeros((halo * bins, cols), jnp.bfloat16)

            @pl.when(jnp.logical_not(has_up))
            def _():
                later_ref[0 : halo * bins, :] = blank

            @pl.when(jnp.logical_not(has_down))
            def _():
                later_ref[(tiles + halo) * bins : total * bins, :] = blank

    to_side.wait_send()

    @pl.when(has_up)
    def _():
        for one in to_up:
            one.wait_send()

    @pl.when(has_down)
    def _():
        for one in to_down:
            one.wait_send()


def on_device(
    tsdf_prior, prior_weight, depth_maps, confidence, frustum_tiles, pixel_index, conv_weights
):
    tiles, bins, cols = tsdf_prior.shape
    owners, cap = frustum_tiles.shape[1:]
    layers = conv_weights.shape[0]
    pixels = depth_maps.shape[1]
    f32 = jnp.float32
    got, ids = pl.pallas_call(
        sample_kernel,
        out_shape=(jax.ShapeDtypeStruct((owners, 3 * cap, cols), f32),
                   jax.ShapeDtypeStruct((owners, cap, cols), jnp.int32)),
        in_specs=[pl.BlockSpec(memory_space=pltpu.HBM)] * 4,
        out_specs=tuple(vmem_specs(2)),
        scratch_shapes=[
            VMEM((owners, cap, LANES), jnp.int32),
            VMEM((pixels // LANES, LANES), f32),
            VMEM((pixels // LANES, LANES), f32),
            VMEM((cap, owners), jnp.int32),
            VMEM((3 * LANES, pixels // LANES), jnp.bfloat16),
            VMEM((owners, 3 * cap, cols), f32),
            pltpu.SemaphoreType.DMA((4,)),
            pltpu.SemaphoreType.DMA((owners - 1,)),
            pltpu.SemaphoreType.DMA((owners - 1,)),
        ],
        compiler_params=pltpu.CompilerParams(collective_id=1, has_side_effects=True, vmem_limit_bytes=20 << 20),
        cost_estimate=pl.CostEstimate(
            flops=6 * LANES * pixels // LANES * owners * cap * cols, bytes_accessed=8 * pixels, transcendentals=0),
        name="sample",
    )(*(pltpu.with_memory_space_constraint(one, pltpu.HBM) for one in (
        pixel_index[0], depth_maps.reshape(-1, LANES), confidence.reshape(-1, LANES), frustum_tiles[0].T)))
    side = lax.axis_index("col").astype(jnp.int32).reshape(1)
    field = jax.ShapeDtypeStruct((tiles, bins, cols), f32)
    joined, new_weight, packed = pl.pallas_call(
        functools.partial(join_kernel, layers),
        out_shape=(field, field, jax.ShapeDtypeStruct((bins, cols), f32)),
        in_specs=[pl.BlockSpec(memory_space=pltpu.SMEM)] * 2 + vmem_specs(3),
        out_specs=tuple(vmem_specs(3)),
        compiler_params=pltpu.CompilerParams(vmem_limit_bytes=20 << 20),
        name="join",
    )(ids, side, got, tsdf_prior, prior_weight)
    total_rows = tiles + 2 * layers
    wide = -(-total_rows * (2 * layers - 1) // cols) * cols
    refined = pl.pallas_call(
        functools.partial(refine_kernel, layers),
        out_shape=field,
        in_specs=vmem_specs(3),
        out_specs=pl.BlockSpec(memory_space=VMEM),
        scratch_shapes=[
            VMEM((2, layers, bins, cols), f32),
            VMEM((5, bins, cols), f32),
            VMEM((total_rows * bins, cols), f32),
            VMEM((total_rows * bins, cols), jnp.bfloat16),
            VMEM((total_rows * bins, cols), jnp.bfloat16),
            VMEM((layers, 6 * bins, 4 * bins), jnp.bfloat16),
            VMEM((layers, 2 * bins, 9 * bins), jnp.bfloat16),
            VMEM((bins, wide), f32),
            VMEM((layers, bins, cols), f32),
            pltpu.SemaphoreType.DMA((7,)),
            pltpu.SemaphoreType.DMA((7,)),
        ],
        compiler_params=pltpu.CompilerParams(collective_id=0, has_side_effects=True, vmem_limit_bytes=20 << 20),
        name="refine",
    )(joined, packed, conv_weights.transpose(0, 3, 4, 2, 1))
    return (refined, new_weight)


def solution(mesh):
    placed = (
        P("row", None, "col"),
        P("row", None, "col"),
        P("row", None),
        P("row", None),
        P(("row", "col"), None, None),
        P(("row", "col"), None, None, None),
        P(),
    )
    return jax.shard_map(
        on_device,
        mesh=mesh,
        in_specs=placed,
        out_specs=(P("row", None, "col"), P("row", None, "col")),
        check_vma=False,
    )
```

```python
import functools

import jax
import jax.numpy as jnp
from jax import lax
from jax.experimental import pallas as pl
from jax.experimental.pallas import tpu as pltpu
from jax.sharding import PartitionSpec as P

GROUPS = 4
TRUNC = 4
LANES = 128
VMEM = pltpu.VMEM
CORNER = 16
UNROLL_ROWS = 4


def vmem_specs(count):
    return [pl.BlockSpec(memory_space=VMEM)] * count


def sample_kernel(places_hbm, depth_hbm, conf_hbm, want_hbm, got_ref, ids_ref,
                  places_ref, depth_ref, conf_ref, want_ref, table_ref, staged_ref,
                  in_sems, send_sems, recv_sems):
    loads = [pltpu.make_async_copy(src, dst, in_sems.at[i]) for i, (src, dst) in enumerate(
        ((depth_hbm, depth_ref), (conf_hbm, conf_ref), (places_hbm, places_ref), (want_hbm, want_ref)))]
    for load in loads:
        load.start()
    owners, cap, _ = places_ref.shape
    depth_rows = depth_ref.shape[0]
    split = lax.axis_size("col")
    me = lax.axis_index("row") * split + lax.axis_index("col")
    barrier = pltpu.get_barrier_semaphore()

    def wrapped(place):
        return jnp.where(place >= owners, place - owners, place)

    def coordinates(place):
        return (place // split, place % split)

    def greet(k, carry):
        pl.semaphore_signal(barrier, inc=1, device_id=coordinates(wrapped(me + 1 + k)),
                            device_id_type=pl.DeviceIdType.MESH)
        return carry

    lax.fori_loop(0, owners - 1, greet, 0)
    for load in loads:
        load.wait()
    for at in range(0, depth_rows, LANES):
        block = depth_ref[at : at + LANES, :].T
        high = block.astype(jnp.bfloat16)
        table_ref[0:LANES, at : at + LANES] = high
        table_ref[LANES : 2 * LANES, at : at + LANES] = (block - high.astype(jnp.float32)).astype(jnp.bfloat16)
        table_ref[2 * LANES : 3 * LANES, at : at + LANES] = conf_ref[at : at + LANES, :].T.astype(jnp.bfloat16)
    want = want_ref[...].astype(jnp.float32)
    listed_by = lax.broadcasted_iota(jnp.int32, want.shape, 1)
    wide = cap * LANES

    def compute(k):
        owner = wrapped(me + 1 + k)
        listed = places_ref[owner]
        index = jnp.concatenate([listed[s : s + 1, :] for s in range(cap)], axis=1)
        row = index // LANES
        lane = index % LANES
        hot = (lax.broadcasted_iota(jnp.int32, (depth_rows, wide), 0) == row)
        hot = hot.astype(jnp.float32).astype(jnp.bfloat16)
        found = jnp.dot(table_ref[...], hot, preferred_element_type=jnp.float32)
        chosen = lax.broadcasted_iota(jnp.int32, (LANES, wide), 0) == lane
        results = []
        for value in (found[0:LANES] + found[LANES : 2 * LANES], found[2 * LANES : 3 * LANES]):
            value = jnp.sum(jnp.where(chosen, value, 0.0), axis=0, keepdims=True)
            results += [value[:, s * LANES : (s + 1) * LANES] for s in range(cap)]
        tile = jnp.sum(jnp.where(listed_by == owner, want, 0.0), axis=1, keepdims=True)
        results.append(jnp.broadcast_to(tile, (cap, LANES)))
        return owner, jnp.concatenate(results, axis=0)

    def copy(k):
        owner = wrapped(me + 1 + k)
        return pltpu.make_async_remote_copy(
            src_ref=staged_ref.at[owner], dst_ref=got_ref.at[me],
            send_sem=send_sems.at[k], recv_sem=recv_sems.at[k],
            device_id=coordinates(owner), device_id_type=pl.DeviceIdType.MESH)

    def arrival(k):
        sender = wrapped(me + owners - 1 - k)
        return pltpu.make_async_remote_copy(
            src_ref=staged_ref.at[sender], dst_ref=got_ref.at[sender],
            send_sem=send_sems.at[k], recv_sem=recv_sems.at[k],
            device_id=coordinates(sender), device_id_type=pl.DeviceIdType.MESH)

    def stage(k):
        pairs = [compute(k), compute(k + 1)]
        for owner, value in pairs:
            staged_ref[owner] = value

    stage(0)
    pl.semaphore_wait(barrier, owners - 1)

    def step(p, carry):
        copy(2 * p - 2).start()
        copy(2 * p - 1).start()
        stage(2 * p)
        return carry

    lax.fori_loop(1, owners // 2, step, 0)
    copy(owners - 2).start()
    got_ref[me] = staged_ref[me]

    def drain(k, carry):
        copy(k).wait_send()
        arrival(k).wait_recv()
        return carry

    lax.fori_loop(0, owners - 1, drain, 0)
    ids_ref[...] = got_ref[:, 2 * cap : 3 * cap, :].astype(jnp.int32)


def join_kernel(halo, ids_ref, side_ref, got_ref, prior_ref, weight_ref, joined_ref, total_ref, packed_ref,
                edge_ref, corner_ref):
    tiles, bins, cols = prior_ref.shape
    readers, rows, _ = got_ref.shape
    cap = rows // 3

    def begin(t, carry):
        weight = weight_ref[t]
        total_ref[t] = weight
        joined_ref[t] = weight * prior_ref[t]
        return carry

    lax.fori_loop(0, tiles, begin, 0, unroll=4)
    levels = lax.broadcasted_iota(jnp.int32, (bins, cols), 0).astype(jnp.float32)

    batch = 2

    def add(step, carry):
        terms = []
        for one in range(batch):
            reader = step * batch + one
            for s in range(cap):
                listed = ids_ref[reader, s, 0]
                tile = jnp.maximum(listed, 0)
                height = got_ref[reader, s : s + 1, :]
                sure = got_ref[reader, cap + s : cap + s + 1, :]
                sure = jnp.where(listed >= 0, sure, 0.0)
                scaled = (height - levels) * (1.0 / TRUNC)
                signed = jnp.clip(scaled, -1.0, 1.0)
                visible = jnp.clip(scaled + 2.0, 0.0, 1.0)
                miss = signed - prior_ref[tile]
                observed = sure * visible / (1.0 + 4.0 * miss * miss)
                terms.append((tile, observed, observed * signed))
        for tile, observed, weighted in terms:
            total_ref[tile] += observed
            joined_ref[tile] += weighted
        return carry

    lax.fori_loop(0, readers // batch, add, 0)
    place = lax.broadcasted_iota(jnp.int32, (bins, cols), 1)
    first = side_ref[0] == 0

    def finish(t, packed):
        value = joined_ref[t] / total_ref[t]
        joined_ref[t] = value
        shift = halo * t + jnp.where(first, halo, 0)
        shift = jnp.where(shift >= cols, shift - cols, shift)
        moved = pltpu.roll(value, shift, 1)
        here = (place >= halo * t) & (place < halo * t + halo)
        return jnp.where(here, moved, packed)

    packed = lax.fori_loop(0, tiles, finish, jnp.zeros((bins, cols), jnp.float32), unroll=4)
    packed_ref[...] = packed
    for i in range(halo):
        edge_ref[0, i] = joined_ref[i].astype(jnp.bfloat16)
        edge_ref[1, i] = joined_ref[tiles - halo + i].astype(jnp.bfloat16)
    turned = packed.T
    corner_ref[0] = turned[0:CORNER].astype(jnp.bfloat16)
    corner_ref[1] = turned[halo * tiles - CORNER : halo * tiles].astype(jnp.bfloat16)


def refine_kernel(layers, joined_ref, packed_ref, edge_ref, corner_ref, kernel_ref, out_ref,
                  edge_rows, edge_cols, corners, cur_ref, even_ref, odd_ref, weights_ref, side_weights_ref,
                  side_ref, gap_ref, send_sems, recv_sems):
    tiles, bins, cols = joined_ref.shape
    halo = layers
    total = tiles + 2 * halo
    row, col = lax.axis_index("row"), lax.axis_index("col")
    has_up = row > 0
    has_down = row < lax.axis_size("row") - 1
    other = 1 - col
    barrier = pltpu.get_barrier_semaphore()

    def greet(device):
        pl.semaphore_signal(barrier, inc=1, device_id=device, device_id_type=pl.DeviceIdType.MESH)

    greet((row, other))

    @pl.when(has_up)
    def _():
        greet((row - 1, col))
        greet((row - 1, other))

    @pl.when(has_down)
    def _():
        greet((row + 1, col))
        greet((row + 1, other))

    pl.semaphore_wait(barrier, 1 + 2 * has_up.astype(jnp.int32) + 2 * has_down.astype(jnp.int32))

    def copy(source, target, slot, device):
        return pltpu.make_async_remote_copy(
            src_ref=source, dst_ref=target, send_sem=send_sems.at[slot], recv_sem=recv_sems.at[slot],
            device_id=device, device_id_type=pl.DeviceIdType.MESH)

    to_side = copy(packed_ref, edge_cols, 2, (row, other))
    to_down = [copy(corner_ref.at[1], corners.at[0], 3, (row + 1, other)),
               copy(edge_ref.at[1], edge_rows.at[0], 0, (row + 1, col))]
    to_up = [copy(corner_ref.at[0], corners.at[1], 4, (row - 1, other)),
             copy(edge_ref.at[0], edge_rows.at[1], 1, (row - 1, col))]
    to_side.start()

    @pl.when(has_up)
    def _():
        for one in to_up:
            one.start()

    @pl.when(has_down)
    def _():
        for one in to_down:
            one.start()

    first = col == 0
    near, far = jnp.where(first, cols - 1, 0), jnp.where(first, 0, cols - 1)
    inward = jnp.where(first, 2, 0)
    lane = lax.broadcasted_iota(jnp.int32, (bins, cols), 1)
    is_near, is_far = lane == near, lane == far

    def silu(v):
        half = 0.5 * v
        return half + half * jnp.tanh(half)

    def put(r, value):
        spot = pl.ds(pl.multiple_of(r * bins, bins), bins)
        cur_ref[spot, :] = value
        even_ref[spot, :] = silu(value).astype(jnp.bfloat16)

    group_in = lax.broadcasted_iota(jnp.int32, (bins, bins), 0) // (bins // GROUPS)
    group_out = lax.broadcasted_iota(jnp.int32, (bins, bins), 1) // (bins // GROUPS)
    empty = jnp.zeros((bins, bins), jnp.bfloat16)

    def widen(layer, carry):
        def dense(dr, dc):
            own = kernel_ref[layer, dr, dc].astype(jnp.float32)
            full = jnp.where(group_in == group_out, jnp.concatenate([own] * GROUPS, axis=0), 0.0)
            return full.T.astype(jnp.bfloat16)

        for at, dc in ((0, 2 - inward), (1, 1), (2, inward)):
            blocks = [dense(dr, dc) for dr in range(3)]
            weights_ref[layer, at * bins : (at + 1) * bins, :] = jnp.concatenate(blocks + [empty], axis=1)
            weights_ref[layer, (3 + at) * bins : (4 + at) * bins, :] = jnp.concatenate([empty] + blocks, axis=1)
        below = [dense(dr, inward) if dc == 1 else empty for dr in range(3) for dc in range(3)]
        side_weights_ref[layer, 0:bins, :] = jnp.concatenate(
            [dense(dr, dc) for dr in range(3) for dc in range(3)], axis=1)
        side_weights_ref[layer, bins : 2 * bins, :] = jnp.concatenate(below, axis=1)
        return carry

    def fill(t, carry):
        put(t + halo, joined_ref[t])
        return carry

    lax.fori_loop(0, layers, widen, 0)
    lax.fori_loop(0, tiles, fill, 0, unroll=4)

    wide = side_ref.shape[1]
    span = 2 * halo - 1
    half_lane = [lane + at for at in range(0, wide, cols)]
    place = [one // span for one in half_lane]
    spot_in = [one % span for one in half_lane]
    mine_low, mine_high = jnp.where(first, 0, halo), jnp.where(first, halo - 1, span)
    mine = [(one >= mine_low) & (one < mine_high) for one in spot_in]
    mine_col = jnp.where(first, 1, -halo)
    side_col = jnp.where(first, 1 - halo, 0)
    shift_in = [one + jnp.where(m, mine_col, side_col) for one, m in zip(spot_in, mine)]

    def lanes_of(value, source):
        return jnp.take_along_axis(value, jnp.minimum(jnp.maximum(source, 0), cols - 1), axis=1)

    to_side.wait_recv()
    for h in range(len(place)):
        source = (place[h] - halo) * halo + shift_in[h]
        value = jnp.where(mine[h], lanes_of(packed_ref[...], source), lanes_of(edge_cols[...], source))
        here = (place[h] >= halo) & (place[h] < halo + tiles)
        side_ref[:, h * cols : (h + 1) * cols] = jnp.where(here, value, 0.0)
    outer = jnp.zeros((bins, cols), jnp.bfloat16)
    odd_ref[0:bins, :] = outer
    odd_ref[(total - 1) * bins : total * bins, :] = outer
    nothing = jnp.zeros((bins, cols), jnp.float32)

    own_col = jnp.where(first, cols - halo + 1, -halo)

    def join_side(edge, corner, base, low):
        turned = jnp.concatenate([corner.astype(jnp.float32), jnp.zeros((cols - CORNER, bins), jnp.float32)], axis=0).T
        for h in range(len(place)):
            if low <= ((h + 1) * cols - 1) // span and low + halo > h * cols // span:
                part = side_ref[:, h * cols : (h + 1) * cols]
                here = jnp.logical_not(mine[h]) & (place[h] >= low) & (place[h] < low + halo)
                part = jnp.where(here, lanes_of(turned, (place[h] - low) * halo + base + shift_in[h]), part)
                for i in range(halo):
                    line = lanes_of(edge[i].astype(jnp.float32), spot_in[h] + own_col)
                    part = jnp.where(mine[h] & (place[h] == low + i), line, part)
                side_ref[:, h * cols : (h + 1) * cols] = part

    @pl.when(has_up)
    def _():
        for one in to_down:
            one.wait_recv()
        join_side(edge_rows[0], corners[0], CORNER - halo * halo, 0)
        for i in range(halo):
            put(i, edge_rows[0, i].astype(jnp.float32))

    @pl.when(jnp.logical_not(has_up))
    def _():
        for i in range(halo):
            put(i, nothing)

    @pl.when(has_down)
    def _():
        for one in to_up:
            one.wait_recv()
        join_side(edge_rows[1], corners[1], 0, halo + tiles)
        for i in range(halo):
            put(tiles + halo + i, edge_rows[1, i].astype(jnp.float32))

    @pl.when(jnp.logical_not(has_down))
    def _():
        for i in range(halo):
            put(tiles + halo + i, nothing)

    wide_place = lax.broadcasted_iota(jnp.int32, (bins, wide), 1) // span
    inside = ((wide_place >= jnp.where(has_up, 0, halo))
              & (wide_place < jnp.where(has_down, total, tiles + halo)))
    middle = span // 2

    def side_step(layer, carry):
        now = side_ref[...]
        active = silu(now)
        shifted = []
        for dr in range(-1, 2):
            for dc in range(-1, 2):
                offset = (-(span * dr + dc)) % wide
                moved = active if offset == 0 else pltpu.roll(active, offset, 1)
                shifted.append(moved.astype(jnp.bfloat16))
        result = jnp.dot(side_weights_ref[layer], jnp.concatenate(shifted, axis=0),
                         preferred_element_type=jnp.float32)
        side_ref[...] = jnp.where(inside, now + result[0:bins], 0.0)
        gap = nothing
        for h in range(len(place)):
            source = lane * span + middle - h * cols
            ok = (source >= 0) & (source < cols)
            moved = jnp.take_along_axis(result[bins : 2 * bins, h * cols : (h + 1) * cols],
                                        jnp.minimum(jnp.maximum(source, 0), cols - 1), axis=1)
            gap = jnp.where(ok, moved, gap)
        gap_ref[layer] = gap
        return carry

    lax.fori_loop(0, layers, side_step, 0)
    inner_shift, outer_shift = jnp.where(first, cols - 1, 1), jnp.where(first, 1, cols - 1)
    pair = 2
    stride = 2 * pair
    for layer in range(layers):
        now_ref, later_ref = (even_ref, odd_ref) if layer % 2 == 0 else (odd_ref, even_ref)
        last = layer == layers - 1
        begin = halo if last else 1
        end = tiles + halo if last else total - 1

        steps = (end - begin) // stride
        unroll = max(u for u in range(1, UNROLL_ROWS + 1) if steps % u == 0)

        def store(r, spot, value):
            if last:
                out_ref[r - halo] = value
            else:
                cur_ref[spot, :] = value
                later_ref[spot, :] = silu(value).astype(jnp.bfloat16)

        def rows(step, carry):
            for one in range(unroll):
                base = begin + step * (stride * unroll) + one * stride
                at = base * bins
                span_rows = (pair + 2) * bins
                window = jnp.concatenate(
                    [now_ref[pl.ds(pl.multiple_of(at - bins + h * pair * bins, bins), span_rows), :]
                     for h in range(2)], axis=1)
                parts = jnp.dot(weights_ref[layer], window, preferred_element_type=jnp.float32)
                for h in range(2):
                    for j in range(pair):
                        part = parts[3 * bins * j : 3 * bins * (j + 1), h * cols : (h + 1) * cols]
                        r = base + h * pair + j
                        shift = near - r
                        gap = pltpu.roll(gap_ref[layer], jnp.where(shift < 0, shift + cols, shift), 1)
                        response = (jnp.where(is_far, 0.0, pltpu.roll(part[0:bins], outer_shift, 1))
                                    + part[bins : 2 * bins]
                                    + jnp.where(is_near, gap, pltpu.roll(part[2 * bins : 3 * bins], inner_shift, 1)))
                        spot = pl.ds(pl.multiple_of(r * bins, bins), bins)
                        value = cur_ref[spot, :] + response
                        store(r, spot, value)
            return carry

        lax.fori_loop(0, steps // unroll, rows, 0)
        if not last:
            blank = jnp.zeros((halo * bins, cols), jnp.bfloat16)

            @pl.when(jnp.logical_not(has_up))
            def _():
                later_ref[0 : halo * bins, :] = blank

            @pl.when(jnp.logical_not(has_down))
            def _():
                later_ref[(tiles + halo) * bins : total * bins, :] = blank

    to_side.wait_send()

    @pl.when(has_up)
    def _():
        for one in to_up:
            one.wait_send()

    @pl.when(has_down)
    def _():
        for one in to_down:
            one.wait_send()


def on_device(
    tsdf_prior, prior_weight, depth_maps, confidence, frustum_tiles, pixel_index, conv_weights
):
    tiles, bins, cols = tsdf_prior.shape
    owners, cap = frustum_tiles.shape[1:]
    layers = conv_weights.shape[0]
    pixels = depth_maps.shape[1]
    f32 = jnp.float32
    got, ids = pl.pallas_call(
        sample_kernel,
        out_shape=(jax.ShapeDtypeStruct((owners, 3 * cap, cols), f32),
                   jax.ShapeDtypeStruct((owners, cap, cols), jnp.int32)),
        in_specs=[pl.BlockSpec(memory_space=pltpu.HBM)] * 4,
        out_specs=tuple(vmem_specs(2)),
        scratch_shapes=[
            VMEM((owners, cap, LANES), jnp.int32),
            VMEM((pixels // LANES, LANES), f32),
            VMEM((pixels // LANES, LANES), f32),
            VMEM((cap, owners), jnp.int32),
            VMEM((3 * LANES, pixels // LANES), jnp.bfloat16),
            VMEM((owners, 3 * cap, cols), f32),
            pltpu.SemaphoreType.DMA((4,)),
            pltpu.SemaphoreType.DMA((owners - 1,)),
            pltpu.SemaphoreType.DMA((owners - 1,)),
        ],
        compiler_params=pltpu.CompilerParams(collective_id=1, has_side_effects=True, vmem_limit_bytes=20 << 20),
        cost_estimate=pl.CostEstimate(
            flops=6 * LANES * pixels // LANES * owners * cap * cols, bytes_accessed=8 * pixels, transcendentals=0),
        name="sample",
    )(*(pltpu.with_memory_space_constraint(one, pltpu.HBM) for one in (
        pixel_index[0], depth_maps.reshape(-1, LANES), confidence.reshape(-1, LANES), frustum_tiles[0].T)))
    side = lax.axis_index("col").astype(jnp.int32).reshape(1)
    field = jax.ShapeDtypeStruct((tiles, bins, cols), f32)
    bf16 = jnp.bfloat16
    joined, new_weight, packed, edge, corner = pl.pallas_call(
        functools.partial(join_kernel, layers),
        out_shape=(field, field, jax.ShapeDtypeStruct((bins, cols), f32),
                   jax.ShapeDtypeStruct((2, layers, bins, cols), bf16),
                   jax.ShapeDtypeStruct((2, CORNER, bins), bf16)),
        in_specs=[pl.BlockSpec(memory_space=pltpu.SMEM)] * 2 + vmem_specs(3),
        out_specs=tuple(vmem_specs(5)),
        compiler_params=pltpu.CompilerParams(vmem_limit_bytes=20 << 20),
        name="join",
    )(ids, side, got, tsdf_prior, prior_weight)
    total_rows = tiles + 2 * layers
    wide = -(-total_rows * (2 * layers - 1) // cols) * cols
    refined = pl.pallas_call(
        functools.partial(refine_kernel, layers),
        out_shape=field,
        in_specs=vmem_specs(5),
        out_specs=pl.BlockSpec(memory_space=VMEM),
        scratch_shapes=[
            VMEM((2, layers, bins, cols), bf16),
            VMEM((bins, cols), f32),
            VMEM((2, CORNER, bins), bf16),
            VMEM((total_rows * bins, cols), f32),
            VMEM((total_rows * bins, cols), jnp.bfloat16),
            VMEM((total_rows * bins, cols), jnp.bfloat16),
            VMEM((layers, 6 * bins, 4 * bins), jnp.bfloat16),
            VMEM((layers, 2 * bins, 9 * bins), jnp.bfloat16),
            VMEM((bins, wide), f32),
            VMEM((layers, bins, cols), f32),
            pltpu.SemaphoreType.DMA((5,)),
            pltpu.SemaphoreType.DMA((5,)),
        ],
        compiler_params=pltpu.CompilerParams(collective_id=0, has_side_effects=True, vmem_limit_bytes=20 << 20),
        name="refine",
    )(joined, packed, edge, corner, conv_weights.transpose(0, 3, 4, 2, 1))
    return (refined, new_weight)


def solution(mesh):
    placed = (
        P("row", None, "col"),
        P("row", None, "col"),
        P("row", None),
        P("row", None),
        P(("row", "col"), None, None),
        P(("row", "col"), None, None, None),
        P(),
    )
    return jax.shard_map(
        on_device,
        mesh=mesh,
        in_specs=placed,
        out_specs=(P("row", None, "col"), P("row", None, "col")),
        check_vma=False,
    )
```
